32 devices in a mesh: gx: 4 (over z), gy: 8 (over y, x, core).
Axes of the slice: x: 2, y: 2, z: 4, core: 2. Of those that a mesh axis runs over, the one named last changes fastest.
Arguments:
- displacement: float32 [3, 128, 5, 1024], P(None, 'gx', None, 'gy'), may hold values from -5 to 5
- velocity: float32 [3, 128, 5, 1024], P(None, 'gx', None, 'gy'), may hold values from -4 to 4
- stiffness: float32 [128, 5, 1024], P('gx', None, 'gy'), may hold values from 0.5 to 2
- inverse_mass: float32 [128, 5, 1024], P('gx', None, 'gy'), may hold values from 0.5 to 2
- facing: int32 [128, 8, 8], P('gx', 'gy'), may hold values from 0 to 1023, as said below
Outputs:
- final_displacement: float32 [3, 128, 5, 1024], P(None, 'gx', None, 'gy')
- final_velocity: float32 [3, 128, 5, 1024], P(None, 'gx', None, 'gy')
The draws below stay inside these ranges and needn't reach their ends.
Inputs may be any that keep to these rules, and one draw needn't show every extreme that they name: facing[x, j, k] names block x' * 8 + j'. For each aligned run of 32 rows x and each j, the 256 entries name blocks with each pair (x' // 32, j') exactly 8 times; repeats are allowed.
All inputs are finite; a program needn't handle non-finite values.
Results may differ from the reference program's by a relative error of at most 0.0001.
Values sent between devices are 32-bit elements; how exact they have to be, the bound alone decides.
A program may use at most 64 MiB of HBM per device.

```python
import math
import jax
import jax.numpy as jnp
from jax import lax

CX = 32
CY = 128
NZ = 5
STEPS = 2
NX = 128
NY = 1024
GROUPS = 8
CAP = 8
DEVICES = 32


def draw_facing(key, part):
    requests = 8 * CX
    seed_list = jax.random.split(key, DEVICES)
    order_list = jax.vmap(lambda seed_one: jax.random.permutation(seed_one, requests))(seed_list)
    target_device = order_list // CAP
    target_row = jax.random.randint(jax.random.fold_in(key, 7), (DEVICES, requests), 0, CX)
    target_row = jnp.where(order_list == 0, 0, target_row)
    target_row = jnp.where(order_list == requests - 1, CX - 1, target_row)
    target_x = target_device // GROUPS * CX + target_row
    numbers = target_x * GROUPS + target_device % GROUPS
    shaped = numbers.reshape(DEVICES // GROUPS, GROUPS, CX, 8).transpose(0, 2, 1, 3)
    return shaped.reshape(NX, GROUPS, 8).astype(jnp.int32)


def block_levels(key, shape, cuts, low, largest):
    def one(axis_at, parts):
        steps = jax.random.uniform(jax.random.fold_in(jax.random.fold_in(key, 6), axis_at), (parts,), jnp.float32, low / len(cuts), largest / len(cuts))
        return jnp.repeat(jnp.exp(steps), shape[axis_at] // parts).reshape((-1,) + (1,) * (len(shape) - axis_at - 1))

    level = one(*cuts[0])
    for cut in cuts[1:]:
        level = level * one(*cut)
    return level


def scatter_about(key, extent, scale, limit, pieces=(), kind=jnp.bfloat16):
    factor_of = block_levels(key, extent, pieces, -0.22, 0.18) if pieces else 1.0
    drawn = jax.random.normal(key, extent, jnp.float32) * scale * factor_of
    return jnp.minimum(jnp.maximum(drawn, -limit), limit).astype(kind)


def setup_inputs(seed: int = 0) -> dict:
    key_of = jax.random.split(jax.random.key(seed), 6)
    displacement = scatter_about(key_of[0], (3, NX, NZ, NY), 1.0, 5.0, ((1, 4), (3, 8)), jnp.float32)
    velocity = scatter_about(key_of[1], (3, NX, NZ, NY), 0.5, 4.0, ((1, 4), (3, 8)), jnp.float32)
    stiffness = jnp.clip(jnp.exp(math.log(2.0) - 1.3862944 * jax.random.uniform(key_of[2], (NX, NZ, NY), jnp.float32) ** block_levels(key_of[2], (NX, NZ, NY), ((0, 4), (2, 8)), -0.2, 0.2)), 0.5, 2.0)
    inverse_mass = jnp.clip(jnp.exp(math.log(2.0) - 1.3862944 * jax.random.uniform(key_of[3], (NX, NZ, NY), jnp.float32) ** block_levels(key_of[3], (NX, NZ, NY), ((0, 4), (2, 8)), -0.2, 0.2)), 0.5, 2.0)
    facing = draw_facing(jax.random.fold_in(key_of[5], 71), 0)
    return dict(displacement=displacement, velocity=velocity, stiffness=stiffness, inverse_mass=inverse_mass, facing=facing)


time_step = 0.2
penalty = 4.0
damping = 1.0
kernel_width = 4.0
frame_extent = 4.0


def block_frame(block_size):
    place = (jnp.arange(block_size, dtype=jnp.float32) - (block_size - 1) / 2.0) * (frame_extent / block_size)
    zero_row = jnp.zeros((block_size,), jnp.float32)
    return jnp.stack([zero_row, place, zero_row], axis=0)


def pair_forces(own_block, facing_blocks):
    block_size = own_block.shape[-1]
    frame = block_frame(block_size)
    own_disp = own_block[:, :3] + frame
    own_vel = own_block[:, 3:]
    far_disp = facing_blocks[:, :, :3] + frame
    far_vel = facing_blocks[:, :, 3:]
    gaps = own_disp[:, None, :, :, None] - far_disp[:, :, :, None, :]
    spread = jnp.sum(gaps * gaps, axis=2)
    weights = jnp.exp(-spread / kernel_width)
    row_total = jnp.sum(weights, axis=3)
    col_total = jnp.sum(weights, axis=2)
    highest = lax.Precision.HIGHEST
    pulled_disp = jnp.einsum("gpij,gpcj->gpci", weights, far_disp, precision=highest)
    pulled_vel = jnp.einsum("gpij,gpcj->gpci", weights, far_vel, precision=highest)
    pushed_disp = jnp.einsum("gpij,gci->gpcj", weights, own_disp, precision=highest)
    pushed_vel = jnp.einsum("gpij,gci->gpcj", weights, own_vel, precision=highest)
    stiff_coef = penalty / (8.0 * block_size)
    damp_coef = damping / (8.0 * block_size)
    row_wide = row_total[:, :, None, :]
    col_wide = col_total[:, :, None, :]
    action = jnp.sum(stiff_coef * (own_disp[:, None] * row_wide - pulled_disp)
                     + damp_coef * (pulled_vel - own_vel[:, None] * row_wide), axis=1)
    reaction = -(stiff_coef * (pushed_disp - far_disp * col_wide)
                 + damp_coef * (far_vel * col_wide - pushed_vel))
    return action, reaction


def internal_force(padded_disp, padded_stiff, displacement):
    size_x, size_z, size_y = displacement.shape[1:]
    corner_sum = jnp.zeros((3, size_x + 1, size_z + 1, size_y + 1), jnp.float32)
    for shift_x in (0, 1):
        for shift_z in (0, 1):
            for shift_y in (0, 1):
                corner_sum = corner_sum + padded_disp[:, shift_x:shift_x + size_x + 1, shift_z:shift_z + size_z + 1, shift_y:shift_y + size_y + 1]
    mean_disp = corner_sum / 8.0
    element_stiff = padded_stiff[:size_x + 1, :size_z + 1, :size_y + 1]
    weighted = element_stiff[None] * mean_disp
    node_stiff = jnp.zeros((size_x, size_z, size_y), jnp.float32)
    node_pull = jnp.zeros((3, size_x, size_z, size_y), jnp.float32)
    for shift_x in (0, 1):
        for shift_z in (0, 1):
            for shift_y in (0, 1):
                node_stiff = node_stiff + element_stiff[shift_x:shift_x + size_x, shift_z:shift_z + size_z, shift_y:shift_y + size_y]
                node_pull = node_pull + weighted[:, shift_x:shift_x + size_x, shift_z:shift_z + size_z, shift_y:shift_y + size_y]
    return node_pull - displacement * node_stiff


def contact_force(displacement, velocity, facing):
    count_x, count_z, count_y = displacement.shape[1:]
    groups = count_y // CY
    blocks = count_x * groups
    surface = jnp.concatenate([displacement[:, :, count_z - 1, :], velocity[:, :, count_z - 1, :]], axis=0)
    blocked = surface.reshape(6, count_x, groups, CY).transpose(1, 2, 0, 3).reshape(blocks, 6, CY)
    targets = facing.reshape(blocks, 8)
    batch_size = 32

    def visit_group(accumulated, group_index):
        first_row = group_index * batch_size
        own_block = lax.dynamic_slice_in_dim(blocked, first_row, batch_size, 0)
        chosen = lax.dynamic_slice_in_dim(targets, first_row, batch_size, 0)
        facing_blocks = blocked[chosen]
        action, reaction = pair_forces(own_block, facing_blocks)
        current = lax.dynamic_slice_in_dim(accumulated, first_row, batch_size, 0)
        accumulated = lax.dynamic_update_slice_in_dim(accumulated, current + action, first_row, 0)
        accumulated = accumulated.at[chosen.reshape(-1)].add(reaction.reshape(batch_size * 8, 3, CY))
        return accumulated, None

    start_total = jnp.zeros((blocks, 3, CY), jnp.float32)
    accumulated, _ = lax.scan(visit_group, start_total, jnp.arange(blocks // batch_size, dtype=jnp.int32))
    return accumulated.reshape(count_x, groups, 3, CY).transpose(2, 0, 1, 3).reshape(3, count_x, count_y)


def reference(displacement, velocity, stiffness, inverse_mass, facing):
    count_x, count_z, count_y = stiffness.shape
    inside = ((jnp.arange(count_x, dtype=jnp.int32) < count_x - 1)[:, None, None]
              & (jnp.arange(count_z, dtype=jnp.int32) < count_z - 1)[None, :, None]
              & (jnp.arange(count_y, dtype=jnp.int32) < count_y - 1)[None, None, :])
    masked_stiff = jnp.where(inside, stiffness, 0.0)
    padded_stiff = jnp.pad(masked_stiff, 1)
    for repeat in range(STEPS):
        padded_disp = jnp.pad(displacement, ((0, 0), (1, 1), (1, 1), (1, 1)))
        internal = internal_force(padded_disp, padded_stiff, displacement)
        contact = contact_force(displacement, velocity, facing)
        total_force = internal.at[:, :, count_z - 1, :].add(contact)
        velocity = velocity + time_step * inverse_mass[None] * total_force
        displacement = displacement + time_step * velocity
    return displacement, velocity
```

```python
import math
import jax
import jax.numpy as jnp
from jax import lax
from jax.experimental import pallas as pl
from jax.experimental.pallas import tpu as pltpu
from jax.sharding import PartitionSpec as P

STEPS = 2

time_step = 0.2
penalty = 4.0
damping = 1.0
kernel_width = 4.0
frame_extent = 4.0

bf16 = jnp.bfloat16
f32 = jnp.float32


def with_halo(cells, sides, width):
    for axis, dim in sides:
        count = lax.axis_size(axis)
        ends = count - 1
        head = lax.slice_in_dim(cells, 0, width, axis=dim)
        tail = lax.slice_in_dim(cells, cells.shape[dim] - width, cells.shape[dim], axis=dim)
        cells = jnp.concatenate(
            [
                lax.ppermute(tail, axis, [(i, (i + 1) % count) for i in range(ends)]),
                cells,
                lax.ppermute(head, axis, [((i + 1) % count, i) for i in range(ends)]),
            ],
            axis=dim,
        )
    return cells


def internal_force(padded_disp, padded_stiff, displacement):
    size_x, size_z, size_y = displacement.shape[1:]
    s = padded_disp[:, 1:] + padded_disp[:, :-1]
    s = s[:, :, 1:] + s[:, :, :-1]
    s = s[:, :, :, 1:] + s[:, :, :, :-1]
    stiff = padded_stiff[: size_x + 1, : size_z + 1, : size_y + 1]
    w = jnp.concatenate([stiff[None] * (s * 0.125), stiff[None]], axis=0)
    w = w[:, 1:] + w[:, :-1]
    w = w[:, :, 1:] + w[:, :, :-1]
    w = w[:, :, :, 1:] + w[:, :, :, :-1]
    return w[:3] - displacement * w[3:]


def split3(x):
    a = x.astype(bf16).astype(f32)
    r = x - a
    b = r.astype(bf16).astype(f32)
    return a, b, r - b


def far_parts(x):
    a, b, c = split3(x)
    rhs = jnp.concatenate([a, b, a, b, c, a], axis=0).astype(bf16)
    lhs = jnp.concatenate([a, b, c, jnp.zeros_like(a)], axis=0).astype(bf16)
    return rhs, lhs


def contact_kernel(rev_row, rev_src, fwd, own_ref, all_ref, out_ref, own_t, acc):
    rows, width = own_ref.shape[0] // 8, own_ref.shape[1]
    row_id = lax.broadcasted_iota(jnp.int32, (8, width), 0)

    @pl.loop(0, rows)
    def _(r):
        x = own_ref[pl.ds(pl.multiple_of(r * 8, 8), 8), :]
        norm = jnp.broadcast_to(x[3:4], x.shape)
        y = jnp.where(row_id < 3, 2.0 * x, jnp.where(row_id == 3, 1.0, jnp.where(row_id == 4, norm, 0.0)))
        a, b, c = split3(y)
        pack = jnp.concatenate([a, a, b, b, a, c], axis=0)
        own_t[r] = pack.T.astype(bf16)

    def pairs(r, blocks):
        parts = [far_parts(all_ref[pl.ds(pl.multiple_of(b * 8, 8), 8), :]) for b in blocks]
        far = jnp.concatenate([p[0] for p in parts], axis=1)
        lhs = jnp.concatenate([p[1] for p in parts], axis=1)
        e = jnp.dot(own_t[r], far, preferred_element_type=f32)
        w = jnp.exp2(e)
        hi = w.astype(bf16)
        lo = (w - hi.astype(f32)).astype(bf16)
        dims = (((1,), (1,)), ((), ()))
        t = lax.dot_general(lhs, hi, dims, preferred_element_type=f32)
        t = t + lax.dot_general(lhs, lo, dims, preferred_element_type=f32)
        return t[0:8] + t[8:16] + t[16:24]

    per_row = fwd.shape[0] // rows

    @pl.loop(0, rows)
    def _(r):
        t = pairs(r, [fwd[r * per_row + k] for k in range(per_row)])
        acc[r] = t

    unroll = 8

    @pl.loop(0, rev_row.shape[0] // unroll)
    def _(g):
        got = []
        for k in range(unroll):
            r = rev_row[g * unroll + k]
            got.append((r, pairs(r, [rev_src[g * unroll + k]])))
        for r, t in got:
            acc[r] = acc[r] + t

    @pl.loop(0, rows)
    def _(r):
        x = own_ref[pl.ds(pl.multiple_of(r * 8, 8), 8), :]
        t = acc[r]
        out_ref[r] = x * t[4:5] - t


def contact_call(rev_row, rev_src, fwd, own, everyone):
    rows, width = own.shape[0] // 8, own.shape[1]
    smem = pl.BlockSpec(memory_space=pltpu.SMEM)
    vmem = pl.BlockSpec(memory_space=pltpu.VMEM)
    return pl.pallas_call(
        contact_kernel,
        out_shape=jax.ShapeDtypeStruct((rows, 8, width), f32),
        in_specs=[smem, smem, smem, vmem, vmem],
        out_specs=vmem,
        scratch_shapes=[
            pltpu.VMEM((rows, width, 48), bf16),
            pltpu.VMEM((rows, 8, width), f32),
        ],
        name="contact",
    )(rev_row, rev_src, fwd, own, everyone)


def local(displacement, velocity, stiffness, inverse_mass, facing):
    count_gx = lax.axis_size("gx")
    count_gy = lax.axis_size("gy")
    devices_all = count_gx * count_gy
    width_x, depth, width_y = stiffness.shape
    global_x = lax.axis_index("gx") * width_x + jnp.arange(width_x, dtype=jnp.int32)
    global_y = lax.axis_index("gy") * width_y + jnp.arange(width_y, dtype=jnp.int32)
    layer_index = jnp.arange(depth, dtype=jnp.int32)
    inside = (
        (global_x < width_x * count_gx - 1)[:, None, None]
        & (layer_index < depth - 1)[None, :, None]
        & (global_y < width_y * count_gy - 1)[None, None, :]
    )
    masked_stiff = jnp.where(inside, stiffness, 0.0)
    per_row = facing.shape[2]
    requests = per_row * width_x
    capacity = requests // devices_all
    me = lax.axis_index("gx") * count_gy + lax.axis_index("gy")
    wanted = facing.reshape(requests)
    wanted_x = wanted // count_gy
    fwd = (wanted_x // width_x * count_gy + wanted % count_gy) * width_x + wanted_x % width_x
    table = lax.all_gather(fwd, ("gx", "gy"))
    mine = table // width_x == me
    ordinal = jnp.arange(requests, dtype=jnp.int32)
    upto = (ordinal[:, None] <= ordinal[None, :]).astype(bf16)
    rank = jnp.dot(mine.astype(bf16), upto, preferred_element_type=f32)
    slot = (jnp.arange(capacity, dtype=jnp.int32) + 1).astype(f32)
    pick = mine[:, None, :] & (rank[:, None, :] == slot[None, :, None])
    rev_row = jnp.sum(jnp.where(pick, (table % width_x)[:, None, :], 0), axis=2).reshape(requests)
    source = jnp.arange(devices_all, dtype=jnp.int32)[:, None] * width_x + (ordinal // per_row)[None, :]
    rev_src = jnp.sum(jnp.where(pick, source[:, None, :], 0), axis=2).reshape(requests)

    place = (jnp.arange(width_y, dtype=f32) - (width_y - 1) / 2.0) * (frame_extent / width_y)
    frame = jnp.stack([jnp.zeros_like(place), place, jnp.zeros_like(place)], axis=0)[:, None, :]
    scale = math.sqrt(math.log2(math.e) / kernel_width)
    stiff_coef = penalty / (8.0 * width_y)
    damp_coef = damping / (8.0 * width_y)

    for repeat in range(STEPS):
        p = displacement[:, :, depth - 1, :] + frame
        q = stiff_coef * p - damp_coef * velocity[:, :, depth - 1, :]
        sp = scale * p
        norm = -jnp.sum(sp * sp, axis=0, keepdims=True)
        surface = jnp.concatenate([sp, norm, jnp.ones_like(norm), q], axis=0).transpose(1, 0, 2)
        surface = surface.reshape(width_x * 8, width_y)
        everyone = lax.all_gather(surface, ("gx", "gy"), tiled=True)
        stacked = jnp.concatenate([displacement, masked_stiff[None]], axis=0)
        padded = with_halo(stacked, (("gx", 1), ("gy", 3)), 1)
        padded = jnp.pad(padded, ((0, 0), (0, 0), (1, 1), (0, 0)))
        internal = internal_force(padded[:3], padded[3], displacement)
        contact = contact_call(rev_row, rev_src, fwd, surface, everyone)
        contact = contact[:, 5:8, :].transpose(1, 0, 2)
        total_force = internal.at[:, :, depth - 1, :].add(contact)
        velocity = velocity + time_step * inverse_mass[None] * total_force
        displacement = displacement + time_step * velocity
    return (displacement, velocity)


def solution(mesh):
    in_specs = (
        P(None, "gx", None, "gy"),
        P(None, "gx", None, "gy"),
        P("gx", None, "gy"),
        P("gx", None, "gy"),
        P("gx", "gy", None),
    )
    out_specs = (P(None, "gx", None, "gy"), P(None, "gx", None, "gy"))
    return jax.shard_map(local, mesh=mesh, in_specs=in_specs, out_specs=out_specs, check_vma=False)
```

```python
import functools
import math
import jax
import jax.numpy as jnp
from jax import lax
from jax.experimental import pallas as pl
from jax.experimental.pallas import tpu as pltpu
from jax.sharding import PartitionSpec as P

STEPS = 2

time_step = 0.2
penalty = 4.0
damping = 1.0
kernel_width = 4.0
frame_extent = 4.0

bf16 = jnp.bfloat16
f32 = jnp.float32


def with_halo(cells, sides, width):
    for axis, dim in sides:
        count = lax.axis_size(axis)
        ends = count - 1
        head = lax.slice_in_dim(cells, 0, width, axis=dim)
        tail = lax.slice_in_dim(cells, cells.shape[dim] - width, cells.shape[dim], axis=dim)
        cells = jnp.concatenate(
            [
                lax.ppermute(tail, axis, [(i, (i + 1) % count) for i in range(ends)]),
                cells,
                lax.ppermute(head, axis, [((i + 1) % count, i) for i in range(ends)]),
            ],
            axis=dim,
        )
    return cells


def internal_force(padded_disp, padded_stiff, displacement):
    size_x, size_z, size_y = displacement.shape[1:]
    s = padded_disp[:, 1:] + padded_disp[:, :-1]
    s = s[:, :, 1:] + s[:, :, :-1]
    s = s[:, :, :, 1:] + s[:, :, :, :-1]
    stiff = padded_stiff[: size_x + 1, : size_z + 1, : size_y + 1]
    w = jnp.concatenate([stiff[None] * (s * 0.125), stiff[None]], axis=0)
    w = w[:, 1:] + w[:, :-1]
    w = w[:, :, 1:] + w[:, :, :-1]
    w = w[:, :, :, 1:] + w[:, :, :, :-1]
    return w[:3] - displacement * w[3:]


def split3(x):
    a = x.astype(bf16).astype(f32)
    r = x - a
    b = r.astype(bf16).astype(f32)
    return a, b, r - b


def far_parts(x):
    a, b, c = split3(x)
    rhs = jnp.concatenate([a, b, a, b, c, a], axis=0).astype(bf16)
    lhs = jnp.concatenate([a, b, c, jnp.zeros_like(a)], axis=0).astype(bf16)
    return rhs, lhs


def contact_kernel(rev_row, rev_src, fwd, own_ref, all_ref, out_ref, own_t, acc):
    rows, width = own_ref.shape[0] // 8, own_ref.shape[1]
    row_id = lax.broadcasted_iota(jnp.int32, (8, width), 0)

    @pl.loop(0, rows)
    def _(r):
        x = own_ref[pl.ds(pl.multiple_of(r * 8, 8), 8), :]
        norm = jnp.broadcast_to(x[3:4], x.shape)
        y = jnp.where(row_id < 3, 2.0 * x, jnp.where(row_id == 3, 1.0, jnp.where(row_id == 4, norm, 0.0)))
        a, b, c = split3(y)
        pack = jnp.concatenate([a, a, b, b, a, c], axis=0)
        own_t[r] = pack.T.astype(bf16)

    def pairs(r, blocks):
        parts = [far_parts(all_ref[pl.ds(pl.multiple_of(b * 8, 8), 8), :]) for b in blocks]
        far = jnp.concatenate([p[0] for p in parts], axis=1)
        lhs = jnp.concatenate([p[1] for p in parts], axis=1)
        e = jnp.dot(own_t[r], far, preferred_element_type=f32)
        w = jnp.exp2(e)
        hi = w.astype(bf16)
        lo = (w - hi.astype(f32)).astype(bf16)
        dims = (((1,), (1,)), ((), ()))
        t = lax.dot_general(lhs, hi, dims, preferred_element_type=f32)
        t = t + lax.dot_general(lhs, lo, dims, preferred_element_type=f32)
        return t[0:8] + t[8:16] + t[16:24]

    per_row = fwd.shape[0] // rows

    @pl.loop(0, rows)
    def _(r):
        t = pairs(r, [fwd[r * per_row + k] for k in range(per_row)])
        acc[r] = t

    unroll = 8

    @pl.loop(0, rev_row.shape[0] // unroll)
    def _(g):
        got = []
        for k in range(unroll):
            r = rev_row[g * unroll + k]
            got.append((r, pairs(r, [rev_src[g * unroll + k]])))
        for r, t in got:
            acc[r] = acc[r] + t

    @pl.loop(0, rows)
    def _(r):
        x = own_ref[pl.ds(pl.multiple_of(r * 8, 8), 8), :]
        t = acc[r]
        out_ref[r] = x * t[4:5] - t


def contact_call(rev_row, rev_src, fwd, own, everyone):
    rows, width = own.shape[0] // 8, own.shape[1]
    smem = pl.BlockSpec(memory_space=pltpu.SMEM)
    vmem = pl.BlockSpec(memory_space=pltpu.VMEM)
    return pl.pallas_call(
        contact_kernel,
        out_shape=jax.ShapeDtypeStruct((rows, 8, width), f32),
        in_specs=[smem, smem, smem, vmem, vmem],
        out_specs=vmem,
        scratch_shapes=[
            pltpu.VMEM((rows, width, 48), bf16),
            pltpu.VMEM((rows, 8, width), f32),
        ],
        name="contact",
    )(rev_row, rev_src, fwd, own, everyone)


def gather_kernel(count_gx, count_gy, own, out, local_sem, send_sems, recv_sems):
    gx = lax.axis_index("gx")
    gy = lax.axis_index("gy")
    bits = count_gy.bit_length() - 1
    flips = [(1 - 2 * ((gy // (1 << k)) % 2)) * (1 << k) for k in range(bits)]
    side = gy % 2
    middle = list(range(1, bits))
    steps = [side * flips[b] + (1 - side) * flips[a] for a, b in zip(middle, middle[::-1])]
    steps.append(flips[0])

    peers = [(lax.rem(gx + k, count_gx), gy) for k in range(1, count_gx)]
    peers += [(gx, gy + step) for step in steps]
    barrier = pltpu.get_barrier_semaphore()
    for peer in peers:
        pl.semaphore_signal(barrier, inc=1, device_id=peer, device_id_type=pl.DeviceIdType.MESH)
    pl.semaphore_wait(barrier, len(peers))

    here = gx * count_gy + gy
    keep = pltpu.make_async_copy(own, out.at[here], local_sem)
    keep.start()
    started = []

    def send(slot, peer):
        copy = pltpu.make_async_remote_copy(
            src_ref=own if slot is None else out.at[slot],
            dst_ref=out.at[here if slot is None else slot],
            send_sem=send_sems.at[len(started)],
            recv_sem=recv_sems.at[here if slot is None else slot],
            device_id=peer,
            device_id_type=pl.DeviceIdType.MESH,
        )
        copy.start()
        started.append(copy)

    def arrived(slot):
        pltpu.make_async_remote_copy(
            src_ref=own,
            dst_ref=out.at[slot],
            send_sem=send_sems.at[0],
            recv_sem=recv_sems.at[slot],
            device_id=peers[0],
            device_id_type=pl.DeviceIdType.MESH,
        ).wait_recv()

    for peer in peers:
        send(None, peer)
    half = 1 << (bits - 1)
    waves = [(k, m) for total in range(count_gx + half - 1) for m in range(half)
             for k in [total - m] if 0 <= k < count_gx and (k, m) != (0, 0)]
    for k, m in waves:
        column = gy
        for b in range(bits - 1):
            if m >> b & 1:
                column = column + steps[b]
        slot = lax.rem(gx + k, count_gx) * count_gy + column
        arrived(slot)
        for b in range(m.bit_length(), bits):
            send(slot, (gx, gy + steps[b]))
    for k, m in [(0, 0)] + waves:
        column = gy + flips[0]
        for b in range(bits - 1):
            if m >> b & 1:
                column = column + steps[bits - 2 - b]
        arrived(lax.rem(gx + k, count_gx) * count_gy + column)
    keep.wait()
    for copy in started:
        copy.wait_send()


def gather_call(own, count_gx, count_gy):
    devices_all = count_gx * count_gy
    bits = count_gy.bit_length() - 1
    half = count_gy // 2
    sends = count_gx - 1 + bits
    for m in range(half):
        sends += (count_gx - (m == 0)) * (bits - m.bit_length())
    return pl.pallas_call(
        functools.partial(gather_kernel, count_gx, count_gy),
        out_shape=jax.ShapeDtypeStruct((devices_all,) + own.shape, f32),
        in_specs=[pl.BlockSpec(memory_space=pltpu.VMEM)],
        out_specs=pl.BlockSpec(memory_space=pl.ANY),
        scratch_shapes=[
            pltpu.SemaphoreType.DMA,
            pltpu.SemaphoreType.DMA((sends,)),
            pltpu.SemaphoreType.DMA((devices_all,)),
        ],
        compiler_params=pltpu.CompilerParams(collective_id=0, has_side_effects=True),
        name="gather",
    )(own)


def local(displacement, velocity, stiffness, inverse_mass, facing):
    count_gx = lax.axis_size("gx")
    count_gy = lax.axis_size("gy")
    devices_all = count_gx * count_gy
    width_x, depth, width_y = stiffness.shape
    global_x = lax.axis_index("gx") * width_x + jnp.arange(width_x, dtype=jnp.int32)
    global_y = lax.axis_index("gy") * width_y + jnp.arange(width_y, dtype=jnp.int32)
    layer_index = jnp.arange(depth, dtype=jnp.int32)
    inside = (
        (global_x < width_x * count_gx - 1)[:, None, None]
        & (layer_index < depth - 1)[None, :, None]
        & (global_y < width_y * count_gy - 1)[None, None, :]
    )
    masked_stiff = jnp.where(inside, stiffness, 0.0)
    per_row = facing.shape[2]
    requests = per_row * width_x
    capacity = requests // devices_all
    me = lax.axis_index("gx") * count_gy + lax.axis_index("gy")
    wanted = facing.reshape(requests)
    extra = -(-requests // (8 * width_y))
    unit = width_x + extra
    wanted_x = wanted // count_gy
    fwd = (wanted_x // width_x * count_gy + wanted % count_gy) * unit + wanted_x % width_x
    place = (jnp.arange(width_y, dtype=f32) - (width_y - 1) / 2.0) * (frame_extent / width_y)
    frame = jnp.stack([jnp.zeros_like(place), place, jnp.zeros_like(place)], axis=0)[:, None, :]
    scale = math.sqrt(math.log2(math.e) / kernel_width)
    stiff_coef = penalty / (8.0 * width_y)
    damp_coef = damping / (8.0 * width_y)

    for repeat in range(STEPS):
        p = displacement[:, :, depth - 1, :] + frame
        q = stiff_coef * p - damp_coef * velocity[:, :, depth - 1, :]
        sp = scale * p
        norm = -jnp.sum(sp * sp, axis=0, keepdims=True)
        surface = jnp.concatenate([sp, norm, jnp.ones_like(norm), q], axis=0).transpose(1, 0, 2)
        surface = surface.reshape(width_x * 8, width_y)
        tail = jnp.pad(fwd.astype(f32), (0, extra * 8 * width_y - requests)).reshape(extra * 8, width_y)
        everyone = gather_call(jnp.concatenate([surface, tail], axis=0), count_gx, count_gy)
        if repeat == 0:
            table = everyone[:, width_x * 8 :].reshape(devices_all, -1)[:, :requests].astype(jnp.int32)
            mine = table // unit == me
            ordinal = jnp.arange(requests, dtype=jnp.int32)
            upto = (ordinal[:, None] <= ordinal[None, :]).astype(bf16)
            rank = jnp.dot(mine.astype(bf16), upto, preferred_element_type=f32)
            slot = (jnp.arange(capacity, dtype=jnp.int32) + 1).astype(f32)
            pick = mine[:, None, :] & (rank[:, None, :] == slot[None, :, None])
            rev_row = jnp.sum(jnp.where(pick, (table % unit)[:, None, :], 0), axis=2).reshape(requests)
            source = jnp.arange(devices_all, dtype=jnp.int32)[:, None] * unit + (ordinal // per_row)[None, :]
            rev_src = jnp.sum(jnp.where(pick, source[:, None, :], 0), axis=2).reshape(requests)
        everyone = everyone.reshape(-1, width_y)
        stacked = jnp.concatenate([displacement, masked_stiff[None]], axis=0)
        padded = with_halo(stacked, (("gx", 1), ("gy", 3)), 1)
        padded = jnp.pad(padded, ((0, 0), (0, 0), (1, 1), (0, 0)))
        internal = internal_force(padded[:3], padded[3], displacement)
        contact = contact_call(rev_row, rev_src, fwd, surface, everyone)
        contact = contact[:, 5:8, :].transpose(1, 0, 2)
        total_force = internal.at[:, :, depth - 1, :].add(contact)
        velocity = velocity + time_step * inverse_mass[None] * total_force
        displacement = displacement + time_step * velocity
    return (displacement, velocity)


def solution(mesh):
    in_specs = (
        P(None, "gx", None, "gy"),
        P(None, "gx", None, "gy"),
        P("gx", None, "gy"),
        P("gx", None, "gy"),
        P("gx", "gy", None),
    )
    out_specs = (P(None, "gx", None, "gy"), P(None, "gx", None, "gy"))
    return jax.shard_map(local, mesh=mesh, in_specs=in_specs, out_specs=out_specs, check_vma=False)
```

```python
import functools
import math
import jax
import jax.numpy as jnp
from jax import lax
from jax.experimental import pallas as pl
from jax.experimental.pallas import tpu as pltpu
from jax.sharding import PartitionSpec as P

STEPS = 2

time_step = 0.2
penalty = 4.0
damping = 1.0
kernel_width = 4.0
frame_extent = 4.0

bf16 = jnp.bfloat16
f32 = jnp.float32


def with_halo(cells, sides, width):
    for axis, dim in sides:
        count = lax.axis_size(axis)
        ends = count - 1
        head = lax.slice_in_dim(cells, 0, width, axis=dim)
        tail = lax.slice_in_dim(cells, cells.shape[dim] - width, cells.shape[dim], axis=dim)
        cells = jnp.concatenate(
            [
                lax.ppermute(tail, axis, [(i, (i + 1) % count) for i in range(ends)]),
                cells,
                lax.ppermute(head, axis, [((i + 1) % count, i) for i in range(ends)]),
            ],
            axis=dim,
        )
    return cells


def internal_force(padded_disp, padded_stiff, displacement):
    size_x, size_z, size_y = displacement.shape[1:]
    s = padded_disp[:, 1:] + padded_disp[:, :-1]
    s = s[:, :, 1:] + s[:, :, :-1]
    s = s[:, :, :, 1:] + s[:, :, :, :-1]
    stiff = padded_stiff[: size_x + 1, : size_z + 1, : size_y + 1]
    w = jnp.concatenate([stiff[None] * (s * 0.125), stiff[None]], axis=0)
    w = w[:, 1:] + w[:, :-1]
    w = w[:, :, 1:] + w[:, :, :-1]
    w = w[:, :, :, 1:] + w[:, :, :, :-1]
    return w[:3] - displacement * w[3:]


def split3(x):
    a = x.astype(bf16).astype(f32)
    r = x - a
    b = r.astype(bf16).astype(f32)
    return a, b, r - b


def far_parts(x):
    a, b, c = split3(x)
    rhs = jnp.concatenate([a, b, a, b, c, a], axis=0).astype(bf16)
    lhs = jnp.concatenate([a, b, c, jnp.zeros_like(a)], axis=0).astype(bf16)
    return rhs, lhs


def contact_kernel(rev_row, rev_src, fwd, own_ref, all_ref, out_ref, own_t, acc):
    rows, width = own_ref.shape[0] // 8, own_ref.shape[1]
    row_id = lax.broadcasted_iota(jnp.int32, (8, width), 0)

    @pl.loop(0, rows)
    def _(r):
        x = own_ref[pl.ds(pl.multiple_of(r * 8, 8), 8), :]
        norm = jnp.broadcast_to(x[3:4], x.shape)
        y = jnp.where(row_id < 3, 2.0 * x, jnp.where(row_id == 3, 1.0, jnp.where(row_id == 4, norm, 0.0)))
        a, b, c = split3(y)
        pack = jnp.concatenate([a, a, b, b, a, c], axis=0)
        own_t[r] = pack.T.astype(bf16)

    def pairs(r, blocks):
        parts = [far_parts(all_ref[pl.ds(pl.multiple_of(b * 8, 8), 8), :]) for b in blocks]
        far = jnp.concatenate([p[0] for p in parts], axis=1)
        lhs = jnp.concatenate([p[1] for p in parts], axis=1)
        e = jnp.dot(own_t[r], far, preferred_element_type=f32)
        w = jnp.exp2(e)
        hi = w.astype(bf16)
        dims = (((1,), (1,)), ((), ()))
        t = lax.dot_general(hi, lhs, dims, preferred_element_type=f32).T
        return t[0:8] + t[8:16] + t[16:24]

    per_row = fwd.shape[0] // rows

    @pl.loop(0, rows, unroll=2)
    def _(r):
        t = pairs(r, [fwd[r * per_row + k] for k in range(per_row)])
        acc[r] = t

    unroll = 16

    @pl.loop(0, rev_row.shape[0] // unroll)
    def _(g):
        got = []
        for k in range(unroll):
            r = rev_row[g * unroll + k]
            got.append((r, pairs(r, [rev_src[g * unroll + k]])))
        for r, t in got:
            acc[r] = acc[r] + t

    @pl.loop(0, rows)
    def _(r):
        x = own_ref[pl.ds(pl.multiple_of(r * 8, 8), 8), :]
        t = acc[r]
        out_ref[r] = x * t[4:5] - t


def contact_call(rev_row, rev_src, fwd, own, everyone):
    rows, width = own.shape[0] // 8, own.shape[1]
    smem = pl.BlockSpec(memory_space=pltpu.SMEM)
    vmem = pl.BlockSpec(memory_space=pltpu.VMEM)
    return pl.pallas_call(
        contact_kernel,
        out_shape=jax.ShapeDtypeStruct((rows, 8, width), f32),
        in_specs=[smem, smem, smem, vmem, vmem],
        out_specs=vmem,
        scratch_shapes=[
            pltpu.VMEM((rows, width, 48), bf16),
            pltpu.VMEM((rows, 8, width), f32),
        ],
        name="contact",
    )(rev_row, rev_src, fwd, own, everyone)


def gather_kernel(count_gx, count_gy, own, out, local_sem, send_sems, recv_sems):
    gx = lax.axis_index("gx")
    gy = lax.axis_index("gy")
    bits = count_gy.bit_length() - 1
    flips = [(1 - 2 * ((gy // (1 << k)) % 2)) * (1 << k) for k in range(bits)]
    side = gy % 2
    middle = list(range(1, bits))
    steps = [side * flips[b] + (1 - side) * flips[a] for a, b in zip(middle, middle[::-1])]
    steps.append(flips[0])

    peers = [(lax.rem(gx + k, count_gx), gy) for k in range(1, count_gx)]
    peers += [(gx, gy + step) for step in steps]
    barrier = pltpu.get_barrier_semaphore()
    for peer in peers:
        pl.semaphore_signal(barrier, inc=1, device_id=peer, device_id_type=pl.DeviceIdType.MESH)
    pl.semaphore_wait(barrier, len(peers))

    here = gx * count_gy + gy
    keep = pltpu.make_async_copy(own, out.at[here], local_sem)
    keep.start()
    started = []

    def send(slot, peer):
        copy = pltpu.make_async_remote_copy(
            src_ref=own if slot is None else out.at[slot],
            dst_ref=out.at[here if slot is None else slot],
            send_sem=send_sems.at[len(started)],
            recv_sem=recv_sems.at[here if slot is None else slot],
            device_id=peer,
            device_id_type=pl.DeviceIdType.MESH,
        )
        copy.start()
        started.append(copy)

    def arrived(slot):
        pltpu.make_async_remote_copy(
            src_ref=own,
            dst_ref=out.at[slot],
            send_sem=send_sems.at[0],
            recv_sem=recv_sems.at[slot],
            device_id=peers[0],
            device_id_type=pl.DeviceIdType.MESH,
        ).wait_recv()

    for peer in peers:
        send(None, peer)
    half = 1 << (bits - 1)
    waves = [(k, m) for total in range(count_gx + half - 1) for m in range(half)
             for k in [total - m] if 0 <= k < count_gx and (k, m) != (0, 0)]
    for k, m in waves:
        column = gy
        for b in range(bits - 1):
            if m >> b & 1:
                column = column + steps[b]
        slot = lax.rem(gx + k, count_gx) * count_gy + column
        arrived(slot)
        for b in range(m.bit_length(), bits):
            send(slot, (gx, gy + steps[b]))
    for k, m in [(0, 0)] + waves:
        column = gy + flips[0]
        for b in range(bits - 1):
            if m >> b & 1:
                column = column + steps[bits - 2 - b]
        arrived(lax.rem(gx + k, count_gx) * count_gy + column)
    keep.wait()
    for copy in started:
        copy.wait_send()


def gather_call(own, count_gx, count_gy):
    devices_all = count_gx * count_gy
    bits = count_gy.bit_length() - 1
    half = count_gy // 2
    sends = count_gx - 1 + bits
    for m in range(half):
        sends += (count_gx - (m == 0)) * (bits - m.bit_length())
    return pl.pallas_call(
        functools.partial(gather_kernel, count_gx, count_gy),
        out_shape=jax.ShapeDtypeStruct((devices_all,) + own.shape, f32),
        in_specs=[pl.BlockSpec(memory_space=pltpu.VMEM)],
        out_specs=pl.BlockSpec(memory_space=pl.ANY),
        scratch_shapes=[
            pltpu.SemaphoreType.DMA,
            pltpu.SemaphoreType.DMA((sends,)),
            pltpu.SemaphoreType.DMA((devices_all,)),
        ],
        compiler_params=pltpu.CompilerParams(collective_id=0, has_side_effects=True),
        name="gather",
    )(own)


def local(displacement, velocity, stiffness, inverse_mass, facing):
    count_gx = lax.axis_size("gx")
    count_gy = lax.axis_size("gy")
    devices_all = count_gx * count_gy
    width_x, depth, width_y = stiffness.shape
    global_x = lax.axis_index("gx") * width_x + jnp.arange(width_x, dtype=jnp.int32)
    global_y = lax.axis_index("gy") * width_y + jnp.arange(width_y, dtype=jnp.int32)
    layer_index = jnp.arange(depth, dtype=jnp.int32)
    inside = (
        (global_x < width_x * count_gx - 1)[:, None, None]
        & (layer_index < depth - 1)[None, :, None]
        & (global_y < width_y * count_gy - 1)[None, None, :]
    )
    masked_stiff = jnp.where(inside, stiffness, 0.0)
    per_row = facing.shape[2]
    requests = per_row * width_x
    capacity = requests // devices_all
    me = lax.axis_index("gx") * count_gy + lax.axis_index("gy")
    wanted = facing.reshape(requests)
    extra = -(-requests // (8 * width_y))
    unit = width_x + extra
    wanted_x = wanted // count_gy
    fwd = (wanted_x // width_x * count_gy + wanted % count_gy) * unit + wanted_x % width_x
    place = (jnp.arange(width_y, dtype=f32) - (width_y - 1) / 2.0) * (frame_extent / width_y)
    frame = jnp.stack([jnp.zeros_like(place), place, jnp.zeros_like(place)], axis=0)[:, None, :]
    scale = math.sqrt(math.log2(math.e) / kernel_width)
    stiff_coef = penalty / (8.0 * width_y)
    damp_coef = damping / (8.0 * width_y)

    for repeat in range(STEPS):
        p = displacement[:, :, depth - 1, :] + frame
        q = stiff_coef * p - damp_coef * velocity[:, :, depth - 1, :]
        sp = scale * p
        norm = -jnp.sum(sp * sp, axis=0, keepdims=True)
        surface = jnp.concatenate([sp, norm, jnp.ones_like(norm), q], axis=0).transpose(1, 0, 2)
        surface = surface.reshape(width_x * 8, width_y)
        tail = jnp.pad(fwd.astype(f32), (0, extra * 8 * width_y - requests)).reshape(extra * 8, width_y)
        everyone = gather_call(jnp.concatenate([surface, tail], axis=0), count_gx, count_gy)
        if repeat == 0:
            table = everyone[:, width_x * 8 :].reshape(devices_all, -1)[:, :requests].astype(jnp.int32)
            mine = table // unit == me
            ordinal = jnp.arange(requests, dtype=jnp.int32)
            upto = (ordinal[:, None] <= ordinal[None, :]).astype(bf16)
            rank = jnp.dot(mine.astype(bf16), upto, preferred_element_type=f32)
            slot = (jnp.arange(capacity, dtype=jnp.int32) + 1).astype(f32)
            pick = mine[:, None, :] & (rank[:, None, :] == slot[None, :, None])
            rev_row = jnp.sum(jnp.where(pick, (table % unit)[:, None, :], 0), axis=2).reshape(requests)
            source = jnp.arange(devices_all, dtype=jnp.int32)[:, None] * unit + (ordinal // per_row)[None, :]
            rev_src = jnp.sum(jnp.where(pick, source[:, None, :], 0), axis=2).reshape(requests)
        everyone = everyone.reshape(-1, width_y)
        stacked = jnp.concatenate([displacement, masked_stiff[None]], axis=0)
        padded = with_halo(stacked, (("gx", 1), ("gy", 3)), 1)
        padded = jnp.pad(padded, ((0, 0), (0, 0), (1, 1), (0, 0)))
        internal = internal_force(padded[:3], padded[3], displacement)
        contact = contact_call(rev_row, rev_src, fwd, surface, everyone)
        contact = contact[:, 5:8, :].transpose(1, 0, 2)
        total_force = internal.at[:, :, depth - 1, :].add(contact)
        velocity = velocity + time_step * inverse_mass[None] * total_force
        displacement = displacement + time_step * velocity
    return (displacement, velocity)


def solution(mesh):
    in_specs = (
        P(None, "gx", None, "gy"),
        P(None, "gx", None, "gy"),
        P("gx", None, "gy"),
        P("gx", None, "gy"),
        P("gx", "gy", None),
    )
    out_specs = (P(None, "gx", None, "gy"), P(None, "gx", None, "gy"))
    return jax.shard_map(local, mesh=mesh, in_specs=in_specs, out_specs=out_specs, check_vma=False)
```

```python
import functools
import math
import jax
import jax.numpy as jnp
from jax import lax
from jax.experimental import pallas as pl
from jax.experimental.pallas import tpu as pltpu
from jax.sharding import PartitionSpec as P

STEPS = 2

time_step = 0.2
penalty = 4.0
damping = 1.0
kernel_width = 4.0
frame_extent = 4.0

bf16 = jnp.bfloat16
f32 = jnp.float32


def internal_force(padded_disp, padded_stiff, displacement):
    size_x, size_z, size_y = displacement.shape[1:]
    s = padded_disp[:, 1:] + padded_disp[:, :-1]
    s = s[:, :, 1:] + s[:, :, :-1]
    s = s[:, :, :, 1:] + s[:, :, :, :-1]
    stiff = padded_stiff[: size_x + 1, : size_z + 1, : size_y + 1]
    w = jnp.concatenate([stiff[None] * (s * 0.125), stiff[None]], axis=0)
    w = w[:, 1:] + w[:, :-1]
    w = w[:, :, 1:] + w[:, :, :-1]
    w = w[:, :, :, 1:] + w[:, :, :, :-1]
    return w[:3] - displacement * w[3:]


def split3(x):
    a = x.astype(bf16).astype(f32)
    r = x - a
    b = r.astype(bf16).astype(f32)
    return a, b, r - b


def far_parts(x):
    a, b, c = split3(x)
    rhs = jnp.concatenate([a, b, a, b, c, a], axis=0).astype(bf16)
    lhs = jnp.concatenate([a, b, c, jnp.zeros_like(a)], axis=0).astype(bf16)
    return rhs, lhs


def contact_kernel(rev_row, rev_src, fwd, own_ref, all_ref, out_ref, own_t, acc):
    rows, width = own_ref.shape[0] // 8, own_ref.shape[1]
    row_id = lax.broadcasted_iota(jnp.int32, (8, width), 0)

    @pl.loop(0, rows)
    def _(r):
        x = own_ref[pl.ds(pl.multiple_of(r * 8, 8), 8), :]
        norm = jnp.broadcast_to(x[3:4], x.shape)
        y = jnp.where(row_id < 3, 2.0 * x, jnp.where(row_id == 3, 1.0, jnp.where(row_id == 4, norm, 0.0)))
        a, b, c = split3(y)
        pack = jnp.concatenate([a, a, b, b, a, c], axis=0)
        own_t[r] = pack.T.astype(bf16)

    def pairs(r, blocks):
        parts = [far_parts(all_ref[pl.ds(pl.multiple_of(b * 8, 8), 8), :]) for b in blocks]
        far = jnp.concatenate([p[0] for p in parts], axis=1)
        lhs = jnp.concatenate([p[1] for p in parts], axis=1)
        e = jnp.dot(own_t[r], far, preferred_element_type=f32)
        w = jnp.exp2(e)
        hi = w.astype(bf16)
        dims = (((1,), (1,)), ((), ()))
        t = lax.dot_general(hi, lhs, dims, preferred_element_type=f32).T
        return t[0:8] + t[8:16] + t[16:24]

    per_row = fwd.shape[0] // rows

    @pl.loop(0, rows, unroll=4)
    def _(r):
        t = pairs(r, [fwd[r * per_row + k] for k in range(per_row)])
        acc[r] = t

    unroll = 32

    @pl.loop(0, rev_row.shape[0] // unroll)
    def _(g):
        got = []
        for k in range(unroll):
            r = rev_row[g * unroll + k]
            got.append((r, pairs(r, [rev_src[g * unroll + k]])))
        for r, t in got:
            acc[r] = acc[r] + t

    @pl.loop(0, rows)
    def _(r):
        x = own_ref[pl.ds(pl.multiple_of(r * 8, 8), 8), :]
        t = acc[r]
        out_ref[r] = x * t[4:5] - t


def contact_call(rev_row, rev_src, fwd, own, everyone):
    rows, width = own.shape[0] // 8, own.shape[1]
    smem = pl.BlockSpec(memory_space=pltpu.SMEM)
    vmem = pl.BlockSpec(memory_space=pltpu.VMEM)
    return pl.pallas_call(
        contact_kernel,
        out_shape=jax.ShapeDtypeStruct((rows, 8, width), f32),
        in_specs=[smem, smem, smem, vmem, vmem],
        out_specs=vmem,
        scratch_shapes=[
            pltpu.VMEM((rows, width, 48), bf16),
            pltpu.VMEM((rows, 8, width), f32),
        ],
        name="contact",
    )(rev_row, rev_src, fwd, own, everyone)


def edge_pieces(columns):
    tall = -(-columns // 8) * 8
    pieces = []
    start = 0
    for dx in (-1, 0, 1):
        for dy in (-1, 0, 1):
            if (dx, dy) != (0, 0):
                rows = tall if dy == 0 else 8
                pieces.append((dx, dy, start, rows))
                start += rows
    return pieces, start


def gather_kernel(count_gx, count_gy, pieces, own, edges, out, halo, local_sem, send_sems, recv_sems, edge_send, edge_recv):
    gx = lax.axis_index("gx")
    gy = lax.axis_index("gy")
    bits = count_gy.bit_length() - 1
    flips = [(1 - 2 * ((gy // (1 << k)) % 2)) * (1 << k) for k in range(bits)]
    side = gy % 2
    middle = list(range(1, bits))
    steps = [side * flips[b] + (1 - side) * flips[a] for a, b in zip(middle, middle[::-1])]
    steps.append(flips[0])

    peers = [(lax.rem(gx + k, count_gx), gy) for k in range(1, count_gx)]
    peers += [(gx, gy + step) for step in steps]
    around = [
        (lax.rem(gx + dx + count_gx, count_gx), lax.rem(gy + dy + count_gy, count_gy))
        for dx, dy, _, _ in pieces
    ]
    barrier = pltpu.get_barrier_semaphore()
    for peer in peers + around:
        pl.semaphore_signal(barrier, inc=1, device_id=peer, device_id_type=pl.DeviceIdType.MESH)
    pl.semaphore_wait(barrier, len(peers) + len(around))

    here = gx * count_gy + gy
    keep = pltpu.make_async_copy(own, out.at[here], local_sem)
    keep.start()
    started = []

    def send(slot, peer):
        copy = pltpu.make_async_remote_copy(
            src_ref=own if slot is None else out.at[slot],
            dst_ref=out.at[here if slot is None else slot],
            send_sem=send_sems.at[len(started)],
            recv_sem=recv_sems.at[here if slot is None else slot],
            device_id=peer,
            device_id_type=pl.DeviceIdType.MESH,
        )
        copy.start()
        started.append(copy)

    def arrived(slot):
        pltpu.make_async_remote_copy(
            src_ref=own,
            dst_ref=out.at[slot],
            send_sem=send_sems.at[0],
            recv_sem=recv_sems.at[slot],
            device_id=peers[0],
            device_id_type=pl.DeviceIdType.MESH,
        ).wait_recv()

    for peer in peers:
        send(None, peer)
    edge_copies = []
    for n, (dx, dy, start, rows) in enumerate(pieces):
        copy = pltpu.make_async_remote_copy(
            src_ref=edges.at[pl.ds(start, rows)],
            dst_ref=halo.at[pl.ds(start, rows)],
            send_sem=edge_send.at[n],
            recv_sem=edge_recv.at[n],
            device_id=around[n],
            device_id_type=pl.DeviceIdType.MESH,
        )
        copy.start()
        edge_copies.append(copy)
    half = 1 << (bits - 1)
    waves = [(k, m) for total in range(count_gx + half - 1) for m in range(half)
             for k in [total - m] if 0 <= k < count_gx and (k, m) != (0, 0)]
    for k, m in waves:
        column = gy
        for b in range(bits - 1):
            if m >> b & 1:
                column = column + steps[b]
        slot = lax.rem(gx + k, count_gx) * count_gy + column
        arrived(slot)
        for b in range(m.bit_length(), bits):
            send(slot, (gx, gy + steps[b]))
    for k, m in [(0, 0)] + waves:
        column = gy + flips[0]
        for b in range(bits - 1):
            if m >> b & 1:
                column = column + steps[bits - 2 - b]
        arrived(lax.rem(gx + k, count_gx) * count_gy + column)
    keep.wait()
    for copy in edge_copies:
        copy.wait()
    for copy in started:
        copy.wait_send()


def gather_call(own, edges, pieces, count_gx, count_gy):
    devices_all = count_gx * count_gy
    bits = count_gy.bit_length() - 1
    half = count_gy // 2
    sends = count_gx - 1 + bits
    for m in range(half):
        sends += (count_gx - (m == 0)) * (bits - m.bit_length())
    return pl.pallas_call(
        functools.partial(gather_kernel, count_gx, count_gy, pieces),
        out_shape=(
            jax.ShapeDtypeStruct((devices_all,) + own.shape, f32),
            jax.ShapeDtypeStruct(edges.shape, f32),
        ),
        in_specs=[pl.BlockSpec(memory_space=pltpu.VMEM)] * 2,
        out_specs=(pl.BlockSpec(memory_space=pl.ANY), pl.BlockSpec(memory_space=pl.ANY)),
        scratch_shapes=[
            pltpu.SemaphoreType.DMA,
            pltpu.SemaphoreType.DMA((sends,)),
            pltpu.SemaphoreType.DMA((devices_all,)),
            pltpu.SemaphoreType.DMA((len(pieces),)),
            pltpu.SemaphoreType.DMA((len(pieces),)),
        ],
        compiler_params=pltpu.CompilerParams(collective_id=0, has_side_effects=True),
        name="gather",
    )(own, edges)


def pack_edges(stacked, pieces):
    fields, width_x, depth, width_y = stacked.shape
    columns = fields * depth
    sides_y = {-1: stacked[:, :, :, 0], 1: stacked[:, :, :, width_y - 1]}
    parts = []
    for dx, dy, _, rows in pieces:
        x = 0 if dx < 0 else width_x - 1
        if dy == 0:
            part = stacked[:, x].reshape(columns, width_y)
            part = jnp.pad(part, ((0, rows - columns), (0, 0)))
        else:
            part = sides_y[dy] if dx == 0 else sides_y[dy][:, x]
            part = part.reshape(-1)
            part = jnp.pad(part, (0, rows * width_y - part.shape[0])).reshape(rows, width_y)
        parts.append(part)
    return jnp.concatenate(parts, axis=0)


def unpack_edges(halo, stacked, pieces):
    fields, width_x, depth, width_y = stacked.shape
    columns = fields * depth
    got = {}
    for dx, dy, start, rows in pieces:
        part = halo[start : start + rows]
        if dy == 0:
            part = part[:columns].reshape(fields, 1, depth, width_y)
        else:
            tall = width_x if dx == 0 else 1
            part = part.reshape(-1)[: columns * tall].reshape(fields, tall, depth, 1)
        got[-dx, -dy] = part
    got[0, 0] = stacked
    lines = [jnp.concatenate([got[dx, dy] for dx in (-1, 0, 1)], axis=1) for dy in (-1, 0, 1)]
    return jnp.concatenate(lines, axis=3)


def local(displacement, velocity, stiffness, inverse_mass, facing):
    count_gx = lax.axis_size("gx")
    count_gy = lax.axis_size("gy")
    devices_all = count_gx * count_gy
    width_x, depth, width_y = stiffness.shape
    global_x = lax.axis_index("gx") * width_x + jnp.arange(width_x, dtype=jnp.int32)
    global_y = lax.axis_index("gy") * width_y + jnp.arange(width_y, dtype=jnp.int32)
    layer_index = jnp.arange(depth, dtype=jnp.int32)
    inside = (
        (global_x < width_x * count_gx - 1)[:, None, None]
        & (layer_index < depth - 1)[None, :, None]
        & (global_y < width_y * count_gy - 1)[None, None, :]
    )
    masked_stiff = jnp.where(inside, stiffness, 0.0)
    per_row = facing.shape[2]
    requests = per_row * width_x
    capacity = requests // devices_all
    me = lax.axis_index("gx") * count_gy + lax.axis_index("gy")
    wanted = facing.reshape(requests)
    extra = -(-requests // (8 * width_y))
    unit = width_x + extra
    wanted_x = wanted // count_gy
    fwd = (wanted_x // width_x * count_gy + wanted % count_gy) * unit + wanted_x % width_x
    place = (jnp.arange(width_y, dtype=f32) - (width_y - 1) / 2.0) * (frame_extent / width_y)
    frame = jnp.stack([jnp.zeros_like(place), place, jnp.zeros_like(place)], axis=0)[:, None, :]
    scale = math.sqrt(math.log2(math.e) / kernel_width)
    stiff_coef = penalty / (8.0 * width_y)
    damp_coef = damping / (8.0 * width_y)

    pieces, _ = edge_pieces(4 * depth)

    for repeat in range(STEPS):
        p = displacement[:, :, depth - 1, :] + frame
        q = stiff_coef * p - damp_coef * velocity[:, :, depth - 1, :]
        sp = scale * p
        norm = -jnp.sum(sp * sp, axis=0, keepdims=True)
        surface = jnp.concatenate([sp, norm, jnp.ones_like(norm), q], axis=0).transpose(1, 0, 2)
        surface = surface.reshape(width_x * 8, width_y)
        tail = jnp.pad(fwd.astype(f32), (0, extra * 8 * width_y - requests)).reshape(extra * 8, width_y)
        stacked = jnp.concatenate([displacement, masked_stiff[None]], axis=0)
        edges = pack_edges(stacked, pieces)
        everyone, halo = gather_call(
            jnp.concatenate([surface, tail], axis=0), edges, pieces, count_gx, count_gy
        )
        if repeat == 0:
            table = everyone[:, width_x * 8 :].reshape(devices_all, -1)[:, :requests].astype(jnp.int32)
            mine = table // unit == me
            ordinal = jnp.arange(requests, dtype=jnp.int32)
            upto = (ordinal[:, None] <= ordinal[None, :]).astype(bf16)
            rank = jnp.dot(mine.astype(bf16), upto, preferred_element_type=f32)
            slot = (jnp.arange(capacity, dtype=jnp.int32) + 1).astype(f32)
            pick = mine[:, None, :] & (rank[:, None, :] == slot[None, :, None])
            rev_row = jnp.sum(jnp.where(pick, (table % unit)[:, None, :], 0), axis=2).reshape(requests)
            source = jnp.arange(devices_all, dtype=jnp.int32)[:, None] * unit + (ordinal // per_row)[None, :]
            rev_src = jnp.sum(jnp.where(pick, source[:, None, :], 0), axis=2).reshape(requests)
        everyone = everyone.reshape(-1, width_y)
        padded = unpack_edges(halo, stacked, pieces)
        padded = jnp.pad(padded, ((0, 0), (0, 0), (1, 1), (0, 0)))
        internal = internal_force(padded[:3], padded[3], displacement)
        contact = contact_call(rev_row, rev_src, fwd, surface, everyone)
        contact = contact[:, 5:8, :].transpose(1, 0, 2)
        total_force = internal.at[:, :, depth - 1, :].add(contact)
        velocity = velocity + time_step * inverse_mass[None] * total_force
        displacement = displacement + time_step * velocity
    return (displacement, velocity)


def solution(mesh):
    in_specs = (
        P(None, "gx", None, "gy"),
        P(None, "gx", None, "gy"),
        P("gx", None, "gy"),
        P("gx", None, "gy"),
        P("gx", "gy", None),
    )
    out_specs = (P(None, "gx", None, "gy"), P(None, "gx", None, "gy"))
    return jax.shard_map(local, mesh=mesh, in_specs=in_specs, out_specs=out_specs, check_vma=False)
```

```python
import functools
import math
import jax
import jax.numpy as jnp
from jax import lax
from jax.experimental import pallas as pl
from jax.experimental.pallas import tpu as pltpu
from jax.sharding import PartitionSpec as P

STEPS = 2

time_step = 0.2
penalty = 4.0
damping = 1.0
kernel_width = 4.0
frame_extent = 4.0

bf16 = jnp.bfloat16
f32 = jnp.float32


def internal_force(padded_disp, padded_stiff, displacement):
    size_x, size_z, size_y = displacement.shape[1:]
    s = padded_disp[:, 1:] + padded_disp[:, :-1]
    s = s[:, :, 1:] + s[:, :, :-1]
    s = s[:, :, :, 1:] + s[:, :, :, :-1]
    stiff = padded_stiff[: size_x + 1, : size_z + 1, : size_y + 1]
    w = jnp.concatenate([stiff[None] * (s * 0.125), stiff[None]], axis=0)
    w = w[:, 1:] + w[:, :-1]
    w = w[:, :, 1:] + w[:, :, :-1]
    w = w[:, :, :, 1:] + w[:, :, :, :-1]
    return w[:3] - displacement * w[3:]


def split3(x):
    a = x.astype(bf16).astype(f32)
    r = x - a
    b = r.astype(bf16).astype(f32)
    return a, b, r - b


def far_parts(x):
    a, b, c = split3(x)
    rhs = jnp.concatenate([a, b, a, b, c, a], axis=0).astype(bf16)
    lhs = jnp.concatenate([a, b, c, jnp.zeros_like(a)], axis=0).astype(bf16)
    return rhs, lhs


def contact_kernel(rev_row, rev_src, fwd, own_ref, all_ref, out_ref, own_t, acc):
    rows, width = own_ref.shape[0] // 8, own_ref.shape[1]
    row_id = lax.broadcasted_iota(jnp.int32, (8, width), 0)

    @pl.loop(0, rows)
    def _(r):
        x = own_ref[pl.ds(pl.multiple_of(r * 8, 8), 8), :]
        norm = jnp.broadcast_to(x[3:4], x.shape)
        y = jnp.where(row_id < 3, 2.0 * x, jnp.where(row_id == 3, 1.0, jnp.where(row_id == 4, norm, 0.0)))
        a, b, c = split3(y)
        pack = jnp.concatenate([a, a, b, b, a, c], axis=0)
        own_t[r] = pack.T.astype(bf16)

    def pairs(r, blocks):
        parts = [far_parts(all_ref[pl.ds(pl.multiple_of(b * 8, 8), 8), :]) for b in blocks]
        far = jnp.concatenate([p[0] for p in parts], axis=1)
        lhs = jnp.concatenate([p[1] for p in parts], axis=1)
        e = jnp.dot(own_t[r], far, preferred_element_type=f32)
        w = jnp.exp2(e)
        hi = w.astype(bf16)
        dims = (((1,), (1,)), ((), ()))
        t = lax.dot_general(hi, lhs, dims, preferred_element_type=f32).T
        return t[0:8] + t[8:16] + t[16:24]

    per_row = fwd.shape[0] // rows

    @pl.loop(0, rows, unroll=8)
    def _(r):
        t = pairs(r, [fwd[r * per_row + k] for k in range(per_row)])
        acc[r] = t

    unroll = 32

    @pl.loop(0, rev_row.shape[0] // unroll)
    def _(g):
        got = []
        for k in range(unroll):
            r = rev_row[g * unroll + k]
            got.append((r, pairs(r, [rev_src[g * unroll + k]])))
        for r, t in got:
            acc[r] = acc[r] + t

    @pl.loop(0, rows)
    def _(r):
        x = own_ref[pl.ds(pl.multiple_of(r * 8, 8), 8), :]
        t = acc[r]
        out_ref[r] = x * t[4:5] - t


def contact_call(rev_row, rev_src, fwd, own, everyone):
    rows, width = own.shape[0] // 8, own.shape[1]
    smem = pl.BlockSpec(memory_space=pltpu.SMEM)
    vmem = pl.BlockSpec(memory_space=pltpu.VMEM)
    return pl.pallas_call(
        contact_kernel,
        out_shape=jax.ShapeDtypeStruct((rows, 8, width), f32),
        in_specs=[smem, smem, smem, vmem, vmem],
        out_specs=vmem,
        scratch_shapes=[
            pltpu.VMEM((rows, width, 48), bf16),
            pltpu.VMEM((rows, 8, width), f32),
        ],
        name="contact",
    )(rev_row, rev_src, fwd, own, everyone)


def edge_pieces(columns):
    tall = -(-columns // 8) * 8
    pieces = []
    start = 0
    for dx in (-1, 0, 1):
        for dy in (-1, 0, 1):
            if (dx, dy) != (0, 0):
                rows = tall if dy == 0 else 8
                pieces.append((dx, dy, start, rows))
                start += rows
    return pieces, start


def gather_kernel(count_gx, count_gy, pieces, own, edges, out, halo, local_sem, send_sems, recv_sems, edge_send, edge_recv):
    gx = lax.axis_index("gx")
    gy = lax.axis_index("gy")
    bits = count_gy.bit_length() - 1
    flips = [(1 - 2 * ((gy // (1 << k)) % 2)) * (1 << k) for k in range(bits)]
    side = gy % 2
    middle = list(range(1, bits))
    steps = [side * flips[b] + (1 - side) * flips[a] for a, b in zip(middle, middle[::-1])]
    steps.append(flips[0])

    peers = [(lax.rem(gx + k, count_gx), gy) for k in range(1, count_gx)]
    peers += [(gx, gy + step) for step in steps]
    around = [
        (lax.rem(gx + dx + count_gx, count_gx), lax.rem(gy + dy + count_gy, count_gy))
        for dx, dy, _, _ in pieces
    ]
    barrier = pltpu.get_barrier_semaphore()
    for peer in peers + around:
        pl.semaphore_signal(barrier, inc=1, device_id=peer, device_id_type=pl.DeviceIdType.MESH)
    pl.semaphore_wait(barrier, len(peers) + len(around))

    here = gx * count_gy + gy
    keep = pltpu.make_async_copy(own, out.at[here], local_sem)
    keep.start()
    started = []

    def send(slot, peer):
        copy = pltpu.make_async_remote_copy(
            src_ref=own if slot is None else out.at[slot],
            dst_ref=out.at[here if slot is None else slot],
            send_sem=send_sems.at[len(started)],
            recv_sem=recv_sems.at[here if slot is None else slot],
            device_id=peer,
            device_id_type=pl.DeviceIdType.MESH,
        )
        copy.start()
        started.append(copy)

    def arrived(slot):
        pltpu.make_async_remote_copy(
            src_ref=own,
            dst_ref=out.at[slot],
            send_sem=send_sems.at[0],
            recv_sem=recv_sems.at[slot],
            device_id=peers[0],
            device_id_type=pl.DeviceIdType.MESH,
        ).wait_recv()

    for peer in peers:
        send(None, peer)
    edge_copies = []
    for n, (dx, dy, start, rows) in enumerate(pieces):
        copy = pltpu.make_async_remote_copy(
            src_ref=edges.at[pl.ds(start, rows)],
            dst_ref=halo.at[pl.ds(start, rows)],
            send_sem=edge_send.at[n],
            recv_sem=edge_recv.at[n],
            device_id=around[n],
            device_id_type=pl.DeviceIdType.MESH,
        )
        copy.start()
        edge_copies.append(copy)
    half = 1 << (bits - 1)
    waves = [(k, m) for total in range(count_gx + half - 1) for m in range(half)
             for k in [total - m] if 0 <= k < count_gx and (k, m) != (0, 0)]
    for k, m in waves:
        column = gy
        for b in range(bits - 1):
            if m >> b & 1:
                column = column + steps[b]
        slot = lax.rem(gx + k, count_gx) * count_gy + column
        arrived(slot)
        for b in range(m.bit_length(), bits):
            send(slot, (gx, gy + steps[b]))
    for k, m in [(0, 0)] + waves:
        column = gy + flips[0]
        for b in range(bits - 1):
            if m >> b & 1:
                column = column + steps[bits - 2 - b]
        arrived(lax.rem(gx + k, count_gx) * count_gy + column)
    keep.wait()
    for copy in edge_copies:
        copy.wait()
    for copy in started:
        copy.wait_send()


def gather_call(own, edges, pieces, count_gx, count_gy):
    devices_all = count_gx * count_gy
    bits = count_gy.bit_length() - 1
    half = count_gy // 2
    sends = count_gx - 1 + bits
    for m in range(half):
        sends += (count_gx - (m == 0)) * (bits - m.bit_length())
    return pl.pallas_call(
        functools.partial(gather_kernel, count_gx, count_gy, pieces),
        out_shape=(
            jax.ShapeDtypeStruct((devices_all,) + own.shape, f32),
            jax.ShapeDtypeStruct(edges.shape, f32),
        ),
        in_specs=[pl.BlockSpec(memory_space=pltpu.VMEM)] * 2,
        out_specs=(pl.BlockSpec(memory_space=pl.ANY), pl.BlockSpec(memory_space=pl.ANY)),
        scratch_shapes=[
            pltpu.SemaphoreType.DMA,
            pltpu.SemaphoreType.DMA((sends,)),
            pltpu.SemaphoreType.DMA((devices_all,)),
            pltpu.SemaphoreType.DMA((len(pieces),)),
            pltpu.SemaphoreType.DMA((len(pieces),)),
        ],
        compiler_params=pltpu.CompilerParams(collective_id=0, has_side_effects=True),
        name="gather",
    )(own, edges)


def pack_edges(stacked, pieces):
    fields, width_x, depth, width_y = stacked.shape
    columns = fields * depth
    sides_y = {-1: stacked[:, :, :, 0], 1: stacked[:, :, :, width_y - 1]}
    parts = []
    for dx, dy, _, rows in pieces:
        x = 0 if dx < 0 else width_x - 1
        if dy == 0:
            part = stacked[:, x].reshape(columns, width_y)
            part = jnp.pad(part, ((0, rows - columns), (0, 0)))
        else:
            part = sides_y[dy] if dx == 0 else sides_y[dy][:, x]
            part = part.reshape(-1)
            part = jnp.pad(part, (0, rows * width_y - part.shape[0])).reshape(rows, width_y)
        parts.append(part)
    return jnp.concatenate(parts, axis=0)


def unpack_edges(halo, stacked, pieces):
    fields, width_x, depth, width_y = stacked.shape
    columns = fields * depth
    got = {}
    for dx, dy, start, rows in pieces:
        part = halo[start : start + rows]
        if dy == 0:
            part = part[:columns].reshape(fields, 1, depth, width_y)
        else:
            tall = width_x if dx == 0 else 1
            part = part.reshape(-1)[: columns * tall].reshape(fields, tall, depth, 1)
        got[-dx, -dy] = part
    got[0, 0] = stacked
    lines = [jnp.concatenate([got[dx, dy] for dx in (-1, 0, 1)], axis=1) for dy in (-1, 0, 1)]
    return jnp.concatenate(lines, axis=3)


def local(displacement, velocity, stiffness, inverse_mass, facing):
    count_gx = lax.axis_size("gx")
    count_gy = lax.axis_size("gy")
    devices_all = count_gx * count_gy
    width_x, depth, width_y = stiffness.shape
    global_x = lax.axis_index("gx") * width_x + jnp.arange(width_x, dtype=jnp.int32)
    global_y = lax.axis_index("gy") * width_y + jnp.arange(width_y, dtype=jnp.int32)
    layer_index = jnp.arange(depth, dtype=jnp.int32)
    inside = (
        (global_x < width_x * count_gx - 1)[:, None, None]
        & (layer_index < depth - 1)[None, :, None]
        & (global_y < width_y * count_gy - 1)[None, None, :]
    )
    masked_stiff = jnp.where(inside, stiffness, 0.0)
    per_row = facing.shape[2]
    requests = per_row * width_x
    capacity = requests // devices_all
    me = lax.axis_index("gx") * count_gy + lax.axis_index("gy")
    wanted = facing.reshape(requests)
    extra = -(-requests // (8 * width_y))
    unit = width_x + extra
    wanted_x = wanted // count_gy
    fwd = (wanted_x // width_x * count_gy + wanted % count_gy) * unit + wanted_x % width_x
    place = (jnp.arange(width_y, dtype=f32) - (width_y - 1) / 2.0) * (frame_extent / width_y)
    frame = jnp.stack([jnp.zeros_like(place), place, jnp.zeros_like(place)], axis=0)[:, None, :]
    scale = math.sqrt(math.log2(math.e) / kernel_width)
    stiff_coef = penalty / (8.0 * width_y)
    damp_coef = damping / (8.0 * width_y)

    pieces, _ = edge_pieces(4 * depth)

    for repeat in range(STEPS):
        p = displacement[:, :, depth - 1, :] + frame
        q = stiff_coef * p - damp_coef * velocity[:, :, depth - 1, :]
        sp = scale * p
        norm = -jnp.sum(sp * sp, axis=0, keepdims=True)
        surface = jnp.concatenate([sp, norm, jnp.ones_like(norm), q], axis=0).transpose(1, 0, 2)
        surface = surface.reshape(width_x * 8, width_y)
        tail = jnp.pad(fwd.astype(f32), (0, extra * 8 * width_y - requests)).reshape(extra * 8, width_y)
        stacked = jnp.concatenate([displacement, masked_stiff[None]], axis=0)
        edges = pack_edges(stacked, pieces)
        everyone, halo = gather_call(
            jnp.concatenate([surface, tail], axis=0), edges, pieces, count_gx, count_gy
        )
        if repeat == 0:
            table = everyone[:, width_x * 8 :].reshape(devices_all, -1)[:, :requests].astype(jnp.int32)
            mine = table // unit == me
            ordinal = jnp.arange(requests, dtype=jnp.int32)
            upto = (ordinal[:, None] <= ordinal[None, :]).astype(bf16)
            rank = jnp.dot(mine.astype(bf16), upto, preferred_element_type=f32)
            slot = (jnp.arange(capacity, dtype=jnp.int32) + 1).astype(f32)
            pick = mine[:, None, :] & (rank[:, None, :] == slot[None, :, None])
            rev_row = jnp.sum(jnp.where(pick, (table % unit)[:, None, :], 0), axis=2).reshape(requests)
            source = jnp.arange(devices_all, dtype=jnp.int32)[:, None] * unit + (ordinal // per_row)[None, :]
            rev_src = jnp.sum(jnp.where(pick, source[:, None, :], 0), axis=2).reshape(requests)
        everyone = everyone.reshape(-1, width_y)
        padded = unpack_edges(halo, stacked, pieces)
        padded = jnp.pad(padded, ((0, 0), (0, 0), (1, 1), (0, 0)))
        internal = internal_force(padded[:3], padded[3], displacement)
        contact = contact_call(rev_row, rev_src, fwd, surface, everyone)
        contact = contact[:, 5:8, :].transpose(1, 0, 2)
        total_force = internal.at[:, :, depth - 1, :].add(contact)
        velocity = velocity + time_step * inverse_mass[None] * total_force
        displacement = displacement + time_step * velocity
    return (displacement, velocity)


def solution(mesh):
    in_specs = (
        P(None, "gx", None, "gy"),
        P(None, "gx", None, "gy"),
        P("gx", None, "gy"),
        P("gx", None, "gy"),
        P("gx", "gy", None),
    )
    out_specs = (P(None, "gx", None, "gy"), P(None, "gx", None, "gy"))
    return jax.shard_map(local, mesh=mesh, in_specs=in_specs, out_specs=out_specs, check_vma=False)
```
